128 devices in a mesh: band: 4 (over y), sector: 32 (over x, z, core).
Axes of the slice: x: 4, y: 4, z: 4, core: 2. Of those that a mesh axis runs over, the one named last changes fastest.
Arguments:
- grid_cells: bfloat16 [8192, 128, 128], P(('band', 'sector')), may hold values from -6 to 6
- remap_weight: bfloat16 [8192, 2, 128, 128], P(('band', 'sector')), may hold values from -0.15625 to 0.15625
- remap_dest: int32 [8192, 2], P(('band', 'sector')), may hold values from 0 to 127, all different within a row; in each aligned block of 64 rows (0 to 63, 64 to 127, ...) at most 2 rows name the same one
- remap_tile: int32 [8192, 2], P(('band', 'sector')), may hold values from 0 to 11
- w_embed: bfloat16 [128, 1024], replicated, may hold values from -0.5 to 0.5
- norm_gain: float32 [1024], replicated, may hold values from 0.25 to 1.75
- w_query: bfloat16 [1024, 1024], replicated
- w_key: bfloat16 [1024, 1024], replicated
- w_value: bfloat16 [1024, 1024], replicated, may hold values from -0.1875 to 0.1875
- w_out: bfloat16 [1024, 1024], replicated, may hold values from -0.1875 to 0.1875
- neighbours: int32 [8, 192, 9], P('band', 'sector'), may hold values from 0 to 1535, as said below
Outputs:
- layer_out: bfloat16 [8, 192, 128, 1024], P('band', 'sector')
The draws below stay inside these ranges and needn't reach their ends.
Inputs may be any that keep to these rules, and one draw needn't show every extreme that they name: `remap_dest`: within the row-blocks of one device, no device number is named more than 2 times; some number is named exactly 2 times. `neighbours`: entry 0 of a tile is the tile itself; every entry lies at most one tile row and one tile column away, columns counted around the sphere, rows never past the first or last; entries may repeat.
All inputs are finite; a program needn't handle non-finite values.
Results may differ from the reference program's by a relative error of at most 0.0064.
Values may be sent and summed in bfloat16 or wider, within the bound.
A program may use at most 256 MiB of HBM per device.

```python
import math
import jax
import jax.numpy as jnp
import numpy as np
from jax import lax

D = 1024
HEADS = 16
HD = 64
C_IN = 128
TILE = 128
ROWCELLS = 128
TOP = 2
RB_DEV = 64
TR_DEV = 2
TC_DEV = 6
CAP = 2
ROWBLOCKS = 8192
TROWS = 8
TCOLS = 192
N_SECTOR = 32
DEVICES = 128


def query_key_pair(key):
    shared = jax.random.normal(jax.random.fold_in(key, 101), (D, D), jnp.float32) / math.sqrt(D)
    other = jax.random.normal(jax.random.fold_in(key, 202), (D, D), jnp.float32) / math.sqrt(D)
    return (other, shared)


def draw_w_query(key, part):
    return query_key_pair(key)[0].astype(jnp.bfloat16)


def draw_w_key(key, part):
    return query_key_pair(key)[1].astype(jnp.bfloat16)


def draw_neighbours(key, part):
    shape = (TROWS, TCOLS, 9)
    row_step = jax.random.randint(jax.random.fold_in(key, 303), shape, -1, 2)
    col_step = jax.random.randint(jax.random.fold_in(key, 404), shape, -1, 2)
    first = jnp.arange(9)[None, None, :] == 0
    row_step = jnp.where(first, 0, row_step)
    col_step = jnp.where(first, 0, col_step)
    rows = jnp.arange(TROWS)[:, None, None] + row_step
    cols = jnp.arange(TCOLS)[None, :, None] + col_step
    rows = jnp.clip(rows, 0, TROWS - 1)
    cols = jnp.mod(cols, TCOLS)
    return (rows * TCOLS + cols).astype(jnp.int32)


def place_ends(values, rng, least, top_value):
    shape = values.shape
    spot = [jax.random.randint(jax.random.fold_in(rng, axis), (), 0, shape[axis]) for axis in range(len(shape))]
    values = values.at[tuple(spot)].set(least)
    longest = shape.index(max(shape))
    spot[longest] = (spot[longest] + 1) % shape[longest]
    return values.at[tuple(spot)].set(top_value)


def shard_levels(rng, shape, split, smallest, largest):
    level, own = 1.0, jax.random.fold_in(rng, 6)
    for axis_at, shards_of in split:
        steps = jnp.exp(jax.random.uniform(jax.random.fold_in(own, axis_at), (shards_of,), jnp.float32, smallest / len(split), largest / len(split)))
        level = level * jnp.repeat(steps, shape[axis_at] // shards_of).reshape([-1 if axis == axis_at else 1 for axis in range(len(shape))])
    return level


def deal_out(rng, own, number, rows, count, top, limit, lean):
    ranking = jax.random.permutation(rng, count)
    heavy_load, usual = portions_of(count, rows * top, limit, lean, True), portions_of(count, rows * top, limit, lean, False)
    places = jnp.arange(count)

    def named(sizes, rotation):
        used = int((sizes > 0).sum())
        fixed = max(1, used // 4)
        passed = fixed + (places - fixed + rotation * (used - fixed)) % max(1, count - fixed)
        return jnp.zeros((count,), jnp.int32).at[ranking[jnp.where(places < fixed, places, passed)]].set(jnp.asarray(sizes, jnp.int32))

    sizes = jnp.where(number % 4 == 0, named(heavy_load, number // 4), named(usual, number - number // 4 - 1))
    mixed = jax.random.permutation(jax.random.fold_in(own, 3), count)
    giver, sink = mixed[0:count // 2 * 2:2], mixed[1:count // 2 * 2:2]
    slack = jnp.minimum(sizes[giver] - 1, limit - sizes[sink]) // 2
    slack = jnp.where((giver == ranking[0]) | (sink == ranking[0]) | (sizes[sink] == 0), 0, jnp.maximum(slack, 0))
    passed = jax.random.randint(jax.random.fold_in(own, 4), (count // 2,), 0, 1 << 20) % (slack + 1)
    sizes = sizes.at[giver].add(-passed).at[sink].add(passed)
    labels = jnp.searchsorted(jnp.cumsum(sizes), jnp.arange(rows * top), side="right").astype(jnp.int32)
    listing = labels.reshape(top, rows).T
    listing = listing[jax.random.permutation(jax.random.fold_in(own, 1), rows)]
    rotation = jax.random.randint(jax.random.fold_in(own, 2), (rows, 1), 0, top)
    return jnp.take_along_axis(listing, (jnp.arange(top)[None, :] + rotation) % top, axis=1)


def portions_of(number_of, total, most, skew, full):
    weights = [(1 << 20) // math.isqrt(standing ** skew) + 1 for standing in range(1, number_of + 1)]
    largest = most if full else min(most, max(-(-total // number_of), total * weights[0] // sum(weights)))
    least = 1 if total - largest >= number_of - 1 else 0
    holding, rest = [largest] + [least] * (number_of - 1), total - largest - least * (number_of - 1)
    while rest > 0:
        candidates = [i for i in range(1, number_of) if holding[i] < largest] or [i for i in range(1, number_of) if holding[i] < most]
        pool, remaining = sum([weights[i] for i in candidates]), rest
        for i in candidates:
            extra = min(most - holding[i], max(1, remaining * weights[i] // pool), rest)
            holding[i] = holding[i] + extra
            rest = rest - extra
    return np.array(holding)


def gaussian(rng, shape, spread, most, pieces=(), held_as=jnp.bfloat16):
    loudness = shard_levels(rng, shape, pieces, -0.22, 0.18) if pieces else 1.0
    values = jax.random.normal(rng, shape, jnp.float32) * spread * loudness
    return jnp.minimum(jnp.maximum(values, -most), most).astype(held_as)


def setup_inputs(seed: int = 0) -> dict:
    streams_of = jax.random.split(jax.random.key(seed), 12)
    grid_cells = gaussian(streams_of[0], (ROWBLOCKS, ROWCELLS, C_IN), 1.0, 6.0, ((0, 128),))
    remap_weight = gaussian(streams_of[1], (ROWBLOCKS, TOP, ROWCELLS, TILE), (ROWCELLS * RB_DEV * TOP // (TR_DEV * TC_DEV)) ** -0.5, 0.15625, ((0, 128),))
    remap_dest_keys = jax.random.split(jax.random.fold_in(streams_of[2], 1), ROWBLOCKS // RB_DEV)
    remap_dest_turns = jax.random.permutation(jax.random.fold_in(streams_of[2], 3), ROWBLOCKS // RB_DEV)
    remap_dest = jax.vmap(lambda own, number: deal_out(jax.random.fold_in(streams_of[2], 2), own, number, RB_DEV, DEVICES, TOP, CAP, 2))(remap_dest_keys, remap_dest_turns).reshape((ROWBLOCKS, TOP))
    remap_tile = place_ends(jax.random.randint(streams_of[3], (ROWBLOCKS, TOP), 0, TR_DEV * TC_DEV), jax.random.fold_in(streams_of[3], 1), 0, (TR_DEV * TC_DEV) - 1).astype(jnp.int32)
    w_embed = gaussian(streams_of[4], (C_IN, D), C_IN ** -0.5, 0.5)
    norm_gain = jnp.clip(1.0 + 0.15 * jax.random.normal(streams_of[5], (D,), jnp.float32), 0.25, 1.75)
    w_query = draw_w_query(jax.random.fold_in(streams_of[11], 71), 0)
    w_key = draw_w_key(jax.random.fold_in(streams_of[11], 71), 0)
    w_value = gaussian(streams_of[8], (D, D), D ** -0.5, 0.1875)
    w_out = gaussian(streams_of[9], (D, D), D ** -0.5, 0.1875)
    neighbours = draw_neighbours(jax.random.fold_in(streams_of[11], 71), 0)
    return dict(grid_cells=grid_cells, remap_weight=remap_weight, remap_dest=remap_dest, remap_tile=remap_tile, w_embed=w_embed, norm_gain=norm_gain, w_query=w_query, w_key=w_key, w_value=w_value, w_out=w_out, neighbours=neighbours)


def tile_angles(rows, cols, nrows, ncols, tile):
    place = jnp.arange(tile)
    across = (place // 16).astype(jnp.float32)
    along = (place % 16).astype(jnp.float32)
    theta = math.pi * (rows[..., None].astype(jnp.float32) + (across + 0.5) * 16.0 / tile) / nrows
    phi = 2.0 * math.pi * (cols[..., None].astype(jnp.float32) + (along + 0.5) / 16.0) / ncols
    return jnp.stack([theta, phi], axis=-2)

def rotate(values, angles):
    size = values.shape[-1]
    quarter = size // 4
    freq = jnp.arange(1, quarter + 1).astype(jnp.float32)
    theta = angles[..., 0, :][..., :, None, None] * freq
    phi = angles[..., 1, :][..., :, None, None] * freq

    def turn(pairs, angle):
        lower = pairs[..., :quarter]
        upper = pairs[..., quarter:]
        cosine = jnp.cos(angle)
        sine = jnp.sin(angle)
        return jnp.concatenate([lower * cosine - upper * sine, lower * sine + upper * cosine], axis=-1)
    return jnp.concatenate([turn(values[..., :2 * quarter], theta), turn(values[..., 2 * quarter:], phi)], axis=-1)

def reference(grid_cells, remap_weight, remap_dest, remap_tile, w_embed, norm_gain, w_query, w_key, w_value, w_out, neighbours):
    ntile = TROWS * TCOLS
    dest = remap_dest.reshape(-1)
    local = remap_tile.reshape(-1)
    grow = dest // N_SECTOR * TR_DEV + local // TC_DEV
    gcol = dest % N_SECTOR * TC_DEV + local % TC_DEV
    target = (grow * TCOLS + gcol).astype(jnp.int32).reshape(DEVICES, RB_DEV * TOP)
    cells = grid_cells.reshape(DEVICES, RB_DEV, ROWCELLS, C_IN)
    weights = remap_weight.reshape(DEVICES, RB_DEV, TOP, ROWCELLS, TILE)

    def add_block(total, inputs):
        cell, weight, where = inputs
        part = jnp.einsum('rkct,rcf->rktf', weight.astype(jnp.float32), cell.astype(jnp.float32)).astype(jnp.bfloat16)
        part = lax.optimization_barrier(part).astype(jnp.float32)
        return (total.at[where].add(part.reshape(-1, TILE, C_IN)), None)
    total, _ = lax.scan(add_block, jnp.zeros((ntile, TILE, C_IN), jnp.float32), (cells, weights, target))
    remapped = total.astype(jnp.bfloat16).reshape(-1, C_IN)
    embedded = jnp.dot(remapped, w_embed, preferred_element_type=jnp.float32)
    meansq = lax.optimization_barrier(jnp.mean(embedded * embedded, axis=-1, keepdims=True))
    normed = (embedded * lax.rsqrt(meansq + 1e-05) * norm_gain).astype(jnp.bfloat16)
    rows = jnp.repeat(jnp.arange(TROWS), TCOLS)
    cols = jnp.tile(jnp.arange(TCOLS), TROWS)
    angles = tile_angles(rows, cols, TROWS, TCOLS, TILE)
    queries = rotate(jnp.dot(normed, w_query, preferred_element_type=jnp.float32).reshape(ntile, TILE, HEADS, HD), angles).astype(jnp.bfloat16)
    keys = rotate(jnp.dot(normed, w_key, preferred_element_type=jnp.float32).reshape(ntile, TILE, HEADS, HD), angles).astype(jnp.bfloat16)
    values = jnp.dot(normed, w_value, preferred_element_type=jnp.float32).astype(jnp.bfloat16).reshape(ntile, TILE, HEADS, HD)
    table = neighbours.reshape(ntile, 9)

    def one_tile(inputs):
        query, listed = inputs
        near_keys = keys[listed].reshape(9 * TILE, HEADS, HD)
        near_values = values[listed].reshape(9 * TILE, HEADS, HD)
        scores = jnp.einsum('qhd,khd->hqk', query.astype(jnp.float32), near_keys.astype(jnp.float32)) / math.sqrt(HD)
        probs = jax.nn.softmax(scores, axis=-1).astype(jnp.bfloat16)
        mixed = jnp.einsum('hqk,khd->qhd', probs.astype(jnp.float32), near_values.astype(jnp.float32))
        return mixed.astype(jnp.bfloat16).reshape(TILE, D)
    attended = lax.map(one_tile, (queries, table)).reshape(-1, D)
    result = jnp.dot(attended, w_out, preferred_element_type=jnp.float32) + embedded
    return result.astype(jnp.bfloat16).reshape(TROWS, TCOLS, TILE, D)
```

```python
import math

import jax
import jax.numpy as jnp
import numpy as np
from jax import lax
from jax.experimental import pallas as pl
from jax.experimental.pallas import tpu as pltpu
from jax.sharding import PartitionSpec as P

NOWN, NEXT, TILE, D, C = 12, 32, 128, 1024, 128
GROUP = 4

def mega_kernel(idx_ref, row_ref, col_ref, rem_ref, we_ref, gain_ref, wq_ref, wk_ref, wv_ref, wo_ref,
                cr_ref, cc_ref, sr_ref, sc_ref, out_ref, k_scr, v_scr, q_scr, att_scr, cos_scr, sin_scr):
    lane = lax.broadcasted_iota(jnp.int32, (1, 128), 1)
    is_row = (lane & 63) < 32
    is_low = (lane & 31) < 16
    first = lane < 64
    rows = GROUP * TILE

    def rotary(u):
        parts = []
        partner = jnp.where(is_low, pltpu.roll(u, 112, 1), pltpu.roll(u, 16, 1))
        return u * cos_scr[...] + partner * sin_scr[...]

    def project(g, own):
        base = g * GROUP
        for i in range(GROUP):
            r = row_ref[base + i]
            c = col_ref[base + i]
            cos_scr[pl.ds(i * TILE, TILE), :] = jnp.where(is_row, cr_ref[r], cc_ref[c])
            sin_scr[pl.ds(i * TILE, TILE), :] = jnp.where(is_row, sr_ref[r], sc_ref[c])
        rem = rem_ref[pl.ds(base, GROUP)].reshape(rows, C)
        emb = jnp.dot(rem, we_ref[...], preferred_element_type=jnp.float32)
        ms = jnp.mean(emb * emb, axis=-1, keepdims=True)
        normed = (emb * lax.rsqrt(ms + 1e-05) * gain_ref[...]).astype(jnp.bfloat16)
        for n in range(4):
            cols = slice(n * 256, (n + 1) * 256)
            k = jnp.dot(normed, wk_ref[:, cols], preferred_element_type=jnp.float32)
            for h in range(2):
                kk = rotary(k[:, h * 128:(h + 1) * 128]).astype(jnp.bfloat16)
                k_scr[pl.ds(base, GROUP), :, n * 256 + h * 128: n * 256 + (h + 1) * 128] = kk.reshape(GROUP, TILE, 128)
            v = jnp.dot(normed, wv_ref[:, cols], preferred_element_type=jnp.float32).astype(jnp.bfloat16)
            v_scr[pl.ds(base, GROUP), :, cols] = v.reshape(GROUP, TILE, 256)
            if own:
                q = jnp.dot(normed, wq_ref[:, cols], preferred_element_type=jnp.float32)
                for h in range(2):
                    qq = rotary(q[:, h * 128:(h + 1) * 128]).astype(jnp.bfloat16)
                    qq = qq * jnp.asarray(0.125, jnp.bfloat16)
                    zero = jnp.zeros_like(qq)
                    q_scr[pl.ds(base, GROUP), 2 * n + h, :TILE, :] = jnp.where(first, qq, zero).reshape(GROUP, TILE, 128)
                    q_scr[pl.ds(base, GROUP), 2 * n + h, TILE:, :] = jnp.where(first, zero, qq).reshape(GROUP, TILE, 128)

    lax.fori_loop(0, NOWN // GROUP, lambda g, c: (project(g, True), c)[1], 0)
    lax.fori_loop(NOWN // GROUP, NEXT // GROUP, lambda g, c: (project(g, False), c)[1], 0)

    ones = jnp.ones((9 * TILE, 128), jnp.bfloat16)

    def attend(step, carry):
        t = step >> 3
        p = step & 7
        col = pl.ds(pl.multiple_of(p * 128, 128), 128)
        ids = [idx_ref[t * 9 + j] for j in range(9)]
        kcat = jnp.concatenate([k_scr[i, :, col] for i in ids], axis=0)
        s = lax.dot_general(q_scr[t, p], kcat, (((1,), (1,)), ((), ())), preferred_element_type=jnp.float32)
        m = jnp.max(s, axis=-1, keepdims=True)
        w = jnp.exp(s - m).astype(jnp.bfloat16)
        vcat = jnp.concatenate([v_scr[i, :, col] for i in ids], axis=0)
        o = jnp.dot(w, jnp.concatenate([vcat, ones], axis=1), preferred_element_type=jnp.float32)
        o = o[:, :128] / o[:, 128:]
        att_scr[t, :, col] = jnp.where(first, o[:TILE], o[TILE:]).astype(jnp.bfloat16)
        return carry

    lax.fori_loop(0, NOWN * 8, attend, 0)

    def finish(g, carry):
        base = g * GROUP
        att = att_scr[pl.ds(base, GROUP)].reshape(rows, D)
        rem = rem_ref[pl.ds(base, GROUP)].reshape(rows, C)
        for n in range(4):
            cols = slice(n * 256, (n + 1) * 256)
            o = jnp.dot(att, wo_ref[:, cols], preferred_element_type=jnp.float32)
            o = o + jnp.dot(rem, we_ref[:, cols], preferred_element_type=jnp.float32)
            out_ref[pl.ds(base, GROUP), :, cols] = o.astype(jnp.bfloat16).reshape(GROUP, TILE, 256)
        return carry

    lax.fori_loop(0, NOWN // GROUP, finish, 0)


def mega(idx, row_of, col_of, rem, we, gain, wq, wk, wv, wo, cr, cc, sr, sc):
    smem = pl.BlockSpec(memory_space=pltpu.SMEM)
    vmem = pl.BlockSpec(memory_space=pltpu.VMEM)
    return pl.pallas_call(
        mega_kernel,
        out_shape=jax.ShapeDtypeStruct((NOWN, TILE, D), jnp.bfloat16),
        in_specs=[smem] * 3 + [vmem] * 11,
        out_specs=vmem,
        scratch_shapes=[
            pltpu.VMEM((NEXT, TILE, D), jnp.bfloat16),
            pltpu.VMEM((NEXT, TILE, D), jnp.bfloat16),
            pltpu.VMEM((NOWN, 8, 2 * TILE, 128), jnp.bfloat16),
            pltpu.VMEM((NOWN, TILE, D), jnp.bfloat16),
            pltpu.VMEM((GROUP * TILE, 128), jnp.float32),
            pltpu.VMEM((GROUP * TILE, 128), jnp.float32),
        ],
        compiler_params=pltpu.CompilerParams(vmem_limit_bytes=60 << 20),
    )(idx, row_of, col_of, rem, we, gain, wq, wk, wv, wo, cr, cc, sr, sc)


PLACES = (
    [(r, c) for r in (1, 2) for c in range(1, 7)]
    + [(0, c) for c in range(1, 7)]
    + [(3, c) for c in range(1, 7)]
    + [(r, 0) for r in range(4)]
    + [(r, 7) for r in range(4)]
)


def shift(block, axis, periodic, up):
    count = lax.axis_size(axis)
    pairs = [(i, i + 1) for i in range(count - 1)]
    if periodic:
        pairs.append((count - 1, 0))
    if not up:
        pairs = [(b, a) for a, b in pairs]
    return lax.ppermute(block, axis, pairs)


def with_halo(own):
    above = shift(own[1:], "band", False, True)
    below = shift(own[:1], "band", False, False)
    tall = jnp.concatenate([above, own, below], axis=0)
    west = shift(tall[:, 5:], "sector", True, True)
    east = shift(tall[:, :1], "sector", True, False)
    flat = [x.reshape((-1,) + own.shape[2:]) for x in (own, above, below, west, east)]
    return jnp.concatenate(flat, axis=0)


def tile_slots(neighbours, band_at, sect_at, ncols):
    r = neighbours // ncols - band_at * 2 + 1
    c = jnp.mod(neighbours % ncols - sect_at * 6 + 1, ncols)
    slot = (r - 1) * 6 + c - 1
    slot = jnp.where(r == 0, 11 + c, slot)
    slot = jnp.where(r == 3, 17 + c, slot)
    slot = jnp.where(c == 0, 24 + r, slot)
    return jnp.where(c == 7, 28 + r, slot)


def trig_tables(band_at, sect_at, nrows, ncols):
    freq = jnp.arange(1, 17).astype(jnp.float32)
    rows = (band_at * 2 - 1 + jnp.arange(4)).astype(jnp.float32)
    cols = jnp.mod(sect_at * 6 - 1 + jnp.arange(8), ncols).astype(jnp.float32)
    across = jnp.arange(8).astype(jnp.float32)
    along = jnp.arange(16).astype(jnp.float32)
    theta = math.pi * (rows[:, None] + (across + 0.5) * 16.0 / 128) / nrows
    phi = 2.0 * math.pi * (cols[:, None] + (along + 0.5) / 16.0) / ncols
    theta = theta[..., None] * freq
    phi = phi[..., None] * freq
    sign = jnp.asarray(np.array([-1.0, 1.0] * 4, np.float32))

    def spread_row(t, s):
        t = lax.optimization_barrier(t)[:, :, None, None, :] * s[:, None]
        return jnp.broadcast_to(t, (4, 8, 16, 8, 16)).reshape(4, 128, 128)

    def spread_col(t, s):
        t = lax.optimization_barrier(t)[:, None, :, None, :] * s[:, None]
        return jnp.broadcast_to(t, (8, 8, 16, 8, 16)).reshape(8, 128, 128)

    one = jnp.ones_like(sign)
    return (
        spread_row(jnp.cos(theta), one),
        spread_col(jnp.cos(phi), one),
        spread_row(jnp.sin(theta), sign),
        spread_col(jnp.sin(phi), sign),
    )


def body(
    grid_cells,
    remap_weight,
    remap_dest,
    remap_tile,
    w_embed,
    norm_gain,
    w_query,
    w_key,
    w_value,
    w_out,
    neighbours,
):
    nband = lax.axis_size("band")
    nsect = lax.axis_size("sector")
    ndev = nband * nsect
    blocks, top, rowcells, tile = remap_weight.shape
    chan = grid_cells.shape[2]
    trows, tcols = (neighbours.shape[0], neighbours.shape[1])
    cap = 2
    items = blocks * top
    parts = jnp.einsum(
        "rkct,rcf->rktf", remap_weight, grid_cells, preferred_element_type=jnp.float32
    )
    parts = parts.astype(jnp.bfloat16).reshape(items, tile, chan)
    dest = remap_dest.reshape(-1)
    local = remap_tile.reshape(-1)
    order = jnp.arange(items)
    earlier = (dest[:, None] == dest[None, :]) & (order[None, :] < order[:, None])
    rank = jnp.sum(earlier.astype(jnp.int32), axis=1)
    slot = dest * cap + rank
    send_parts = jnp.zeros((ndev * cap, tile, chan), jnp.bfloat16).at[slot].set(parts)
    send_ids = jnp.full((ndev * cap,), -1, jnp.int32).at[slot].set(local)
    got_parts, got_ids = (
        lax.all_to_all(send_parts, ("band", "sector"), split_axis=0, concat_axis=0, tiled=True),
        lax.all_to_all(send_ids, ("band", "sector"), split_axis=0, concat_axis=0, tiled=True),
    )
    owned = trows * tcols
    select = (got_ids[None, :] == jnp.arange(owned)[:, None]).astype(jnp.bfloat16)
    remapped = jnp.einsum(
        "ls,stc->ltc", select, got_parts, preferred_element_type=jnp.float32
    ).astype(jnp.bfloat16)
    band_at = lax.axis_index("band")
    sect_at = lax.axis_index("sector")
    nrows = trows * nband
    ncols = tcols * nsect
    tiles = with_halo(remapped.reshape(trows, tcols, tile, chan))
    index = tile_slots(neighbours.reshape(owned, 9), band_at, sect_at, ncols).reshape(-1)
    tables = trig_tables(band_at, sect_at, nrows, ncols)
    row_of = jnp.asarray(np.array([r for r, _ in PLACES], np.int32))
    col_of = jnp.asarray(np.array([c for _, c in PLACES], np.int32))
    result = mega(
        index, row_of, col_of, tiles, w_embed, norm_gain.reshape(1, -1),
        w_query, w_key, w_value, w_out, *tables,
    )
    return result.reshape(trows, tcols, tile, -1)


def solution(mesh):
    return jax.shard_map(
        body,
        mesh=mesh,
        in_specs=(
            P(("band", "sector"), None, None),
            P(("band", "sector"), None, None, None),
            P(("band", "sector"), None),
            P(("band", "sector"), None),
            P(),
            P(),
            P(),
            P(),
            P(),
            P(),
            P("band", "sector", None),
        ),
        out_specs=P("band", "sector", None, None),
        check_vma=False,
    )
```

```python
import functools
import math

import jax
import jax.numpy as jnp
import numpy as np
from jax import lax
from jax.experimental import pallas as pl
from jax.experimental.pallas import tpu as pltpu
from jax.sharding import PartitionSpec as P

NOWN, NEXT, TILE, D, C = 12, 32, 128, 1024, 128
CHUNKS = 4
TOK = TILE // CHUNKS
STRIDE = 37

PLACES = (
    [(r, c) for r in (1, 2) for c in range(1, 7)]
    + [(0, c) for c in range(1, 7)]
    + [(3, c) for c in range(1, 7)]
    + [(r, 0) for r in range(4)]
    + [(r, 7) for r in range(4)]
)


def front_kernel(nband, nsect, item_ref, valid_ref, ids_ref, gain_ref, cr_ref, cc_ref, sr_ref, sc_ref,
                 cells_hbm, weight_hbm, we_hbm, wq_hbm, wk_hbm, wv_hbm,
                 rem_out, q_out, k_out, v_out,
                 cells_ref, weight_ref, we_ref, wq_ref, wk_ref, wv_ref,
                 send_scr, recv_scr, gids_scr, lhs_scr, rem_scr, q_scr, k_scr, v_scr,
                 load_sem, out_sem, send_sem, recv_sem, isend_sem, irecv_sem, hsend_sem, hrecv_sem):
    ndev = nband * nsect
    band, sect = lax.axis_index("band"), lax.axis_index("sector")
    me = band * nsect + sect
    mesh_id = pl.DeviceIdType.MESH
    loads = [
        pltpu.make_async_copy(src, dst, load_sem.at[i])
        for i, (src, dst) in enumerate((
            (cells_hbm, cells_ref), (weight_hbm, weight_ref), (we_hbm, we_ref),
            (wk_hbm, wk_ref), (wv_hbm, wv_ref), (wq_hbm, wq_ref)))
    ]
    loads[0].start()
    loads[1].start()
    barrier = pltpu.get_barrier_semaphore()

    def where_is(i):
        d = lax.rem(me + i * STRIDE, ndev)
        return d, (lax.div(d, nsect), lax.rem(d, nsect))

    def greet(i, carry):
        _, place = where_is(i)
        pl.semaphore_signal(barrier, inc=1, device_id=place, device_id_type=mesh_id)
        return carry

    lax.fori_loop(1, ndev, greet, 0)
    rem_scr[:, NOWN:] = jnp.zeros((CHUNKS, NEXT - NOWN, TOK, C), jnp.bfloat16)
    loads[0].wait()
    loads[1].wait()
    for load in loads[2:]:
        load.start()

    def fill(dst, slot, d):
        for k in range(2):
            item = item_ref[2 * d + k]
            value = lax.dot_general(weight_ref[item], cells_ref[item >> 1], (((0,), (0,)), ((), ())),
                                    preferred_element_type=jnp.float32)
            value = (value * valid_ref[2 * d + k]).astype(jnp.bfloat16)
            for h in range(CHUNKS):
                dst[h, slot, k] = value[h * TOK:(h + 1) * TOK]

    fill(recv_scr, me, me)
    gids_scr[me] = ids_ref[me]

    def make(i):
        d, _ = where_is(i)
        fill(send_scr, d, d)

    def ship(h, i):
        d, place = where_is(i)
        pltpu.make_async_remote_copy(
            src_ref=send_scr.at[h, d], dst_ref=recv_scr.at[h, me],
            send_sem=send_sem.at[h], recv_sem=recv_sem.at[h],
            device_id=place, device_id_type=mesh_id).start()

    def ship_first(i):
        d, place = where_is(i)
        pltpu.make_async_remote_copy(
            src_ref=ids_ref.at[d], dst_ref=gids_scr.at[me], send_sem=isend_sem, recv_sem=irecv_sem,
            device_id=place, device_id_type=mesh_id).start()
        ship(0, i)

    def ship_all(h):
        lax.fori_loop(1, ndev, lambda i, c: (ship(h, i), c)[1], 0)

    make(1)
    make(2)
    pl.semaphore_wait(barrier, ndev - 1)

    def step(i, carry):
        make(i + 2)
        ship_first(i)
        return carry

    lax.fori_loop(1, ndev - 2, step, 0)
    ship_first(ndev - 2)
    ship_first(ndev - 1)
    ship_all(1)

    others = pl.ds(0, ndev - 1)
    pltpu.make_async_copy(gids_scr.at[others], gids_scr.at[others], irecv_sem).wait()
    lane = lax.broadcasted_iota(jnp.int32, (NOWN * 16, 128), 1)
    row = lax.broadcasted_iota(jnp.int32, (NOWN * 16, 128), 0)
    diag = (lane & 15) == (row & 15)
    want = ((row >> 4) + 1).astype(jnp.float32)
    for b in range(ndev // 4):
        named = gids_scr[4 * b] + gids_scr[4 * b + 1] + gids_scr[4 * b + 2] + gids_scr[4 * b + 3]
        hit = jnp.where(diag & (named == want), 1.0, 0.0)
        lhs_scr[:, b * 128:(b + 1) * 128] = hit.astype(jnp.bfloat16)
    for load in loads[2:]:
        load.wait()

    lane = lax.broadcasted_iota(jnp.int32, (1, 128), 1)
    is_row = (lane & 63) < 32
    is_low = (lane & 31) < 16

    north = jnp.maximum(band - 1, 0)
    south = jnp.minimum(band + 1, nband - 1)
    west = lax.rem(sect + nsect - 1, nsect)
    east = lax.rem(sect + 1, nsect)

    def halo(h):
        def send(src, dst, count, place):
            pltpu.make_async_remote_copy(
                src_ref=rem_scr.at[h, pl.ds(src, count)], dst_ref=rem_scr.at[h, pl.ds(dst, count)],
                send_sem=hsend_sem.at[h], recv_sem=hrecv_sem.at[h],
                device_id=place, device_id_type=mesh_id).start()

        send(0, 29, 1, (band, west))
        send(6, 30, 1, (band, west))
        send(5, 25, 1, (band, east))
        send(11, 26, 1, (band, east))

        @pl.when(band > 0)
        def _():
            send(0, 18, 6, (north, sect))
            send(0, 31, 1, (north, west))
            send(5, 27, 1, (north, east))

        @pl.when(band < nband - 1)
        def _():
            send(6, 12, 6, (south, sect))
            send(6, 28, 1, (south, west))
            send(11, 24, 1, (south, east))

    def halo_wait(h, sem):
        def wait(count):
            ref = rem_scr.at[h, pl.ds(0, count)]
            pltpu.make_async_copy(ref, ref, sem).wait()

        inner = (band > 0) & (band < nband - 1)

        @pl.when(inner)
        def _():
            wait(20)

        @pl.when(jnp.logical_not(inner))
        def _():
            wait(12)

    def project(h, base, count):
        rows = count * TOK
        toks = pl.ds(pl.multiple_of(h * TOK, TOK), TOK)
        tiles = slice(base, base + count)
        places = PLACES[base:base + count]
        def spread(row_table, col_table):
            blocks = []
            for r, c in places:
                for g in range(TOK // 16):
                    line = row_table[r, pl.ds(h * (TOK // 16) + g, 1), :]
                    blocks.append(jnp.where(is_row, line, col_table[c]))
            return jnp.concatenate(blocks, axis=0)

        cos, sin = spread(cr_ref, cc_ref), spread(sr_ref, sc_ref)

        def rotary(u):
            partner = jnp.where(is_low, pltpu.roll(u, 112, 1), pltpu.roll(u, 16, 1))
            return u * cos + partner * sin

        rem = rem_scr[h, tiles].reshape(rows, C)
        emb = jnp.dot(rem, we_ref[...], preferred_element_type=jnp.float32)
        ms = jnp.mean(emb * emb, axis=-1, keepdims=True)
        normed = (emb * lax.rsqrt(ms + 1e-05) * gain_ref[...]).astype(jnp.bfloat16)

        def put(dst, pair, value):
            dst[pair, tiles, toks, :] = value.reshape(count, TOK, 128)

        for n in range(4):
            cols = slice(n * 256, (n + 1) * 256)
            k = jnp.dot(normed, wk_ref[:, cols], preferred_element_type=jnp.float32)
            v = jnp.dot(normed, wv_ref[:, cols], preferred_element_type=jnp.float32)
            for p in range(2):
                half = slice(p * 128, (p + 1) * 128)
                put(k_scr, 2 * n + p, rotary(k[:, half]).astype(jnp.bfloat16))
                put(v_scr, 2 * n + p, v[:, half].astype(jnp.bfloat16))
            if base < NOWN:
                q = jnp.dot(normed, wq_ref[:, cols], preferred_element_type=jnp.float32)
                for p in range(2):
                    half = slice(p * 128, (p + 1) * 128)
                    turned = rotary(q[:, half]).astype(jnp.bfloat16)
                    put(q_scr, 2 * n + p, turned * jnp.asarray(0.125, jnp.bfloat16))

    def outs(h):
        toks = pl.ds(pl.multiple_of(h * TOK, TOK), TOK)
        return [
            pltpu.make_async_copy(src.at[:, :, toks, :], dst.at[:, :, toks, :], out_sem.at[h, i])
            for i, (src, dst) in enumerate(((k_scr, k_out), (v_scr, v_out), (q_scr, q_out)))
        ] + [pltpu.make_async_copy(rem_scr.at[h, pl.ds(0, NOWN)], rem_out.at[:, toks, :], out_sem.at[h, 3])]

    def chunk(h, carry):
        pltpu.make_async_copy(recv_scr.at[h, others], recv_scr.at[h, others], recv_sem.at[h]).wait()

        @pl.when(h < CHUNKS - 2)
        def _():
            ship_all(h + 2)

        for b in range(TOK // 32):
            low = recv_scr[h, :, :, b * 32:b * 32 + 16, :].reshape(ndev * 32, 128)
            high = recv_scr[h, :, :, b * 32 + 16:b * 32 + 32, :].reshape(ndev * 32, 128)
            total = jnp.dot(lhs_scr[...], jnp.concatenate([low, high], axis=1),
                            preferred_element_type=jnp.float32).astype(jnp.bfloat16)
            for l in range(NOWN):
                rem_scr[h, l, b * 32:b * 32 + 16, :] = total[l * 16:(l + 1) * 16, :128]
                rem_scr[h, l, b * 32 + 16:b * 32 + 32, :] = total[l * 16:(l + 1) * 16, 128:]
        halo(h)

        @pl.when(h > 0)
        def _():
            for copy in outs(h - 1):
                copy.start()

        project(h, 0, NOWN)
        halo_wait(h, hrecv_sem.at[h])
        project(h, NOWN, NEXT - NOWN)
        return carry

    lax.fori_loop(0, CHUNKS, chunk, 0)
    for copy in outs(CHUNKS - 1):
        copy.start()
    pltpu.make_async_copy(ids_ref.at[others], ids_ref.at[others], isend_sem).wait()
    for h in range(CHUNKS):
        pltpu.make_async_copy(send_scr.at[h, others], send_scr.at[h, others], send_sem.at[h]).wait()
        halo_wait(h, hsend_sem.at[h])
        for copy in outs(h):
            copy.wait()


def front(nband, nsect, item, valid, ids, gain, tables, cells, weights, we, wq, wk, wv):
    ndev = nband * nsect
    smem = pl.BlockSpec(memory_space=pltpu.SMEM)
    vmem = pl.BlockSpec(memory_space=pltpu.VMEM)
    hbm = pl.BlockSpec(memory_space=pltpu.HBM)
    bf16 = jnp.bfloat16
    items, blocks = weights.shape[0], cells.shape[0]
    return pl.pallas_call(
        functools.partial(front_kernel, nband, nsect),
        out_shape=[
            jax.ShapeDtypeStruct((NOWN, TILE, C), bf16),
            jax.ShapeDtypeStruct((8, NOWN, TILE, 128), bf16),
            jax.ShapeDtypeStruct((8, NEXT, TILE, 128), bf16),
            jax.ShapeDtypeStruct((8, NEXT, TILE, 128), bf16),
        ],
        in_specs=[smem, smem] + [vmem] * 6 + [hbm] * 6,
        out_specs=[hbm] * 4,
        scratch_shapes=[
            pltpu.VMEM((blocks, 128, C), bf16),
            pltpu.VMEM((items, 128, TILE), bf16),
            pltpu.VMEM((C, D), bf16),
            pltpu.VMEM((D, D), bf16),
            pltpu.VMEM((D, D), bf16),
            pltpu.VMEM((D, D), bf16),
            pltpu.VMEM((CHUNKS, ndev, 2, TOK, C), bf16),
            pltpu.VMEM((CHUNKS, ndev, 2, TOK, C), bf16),
            pltpu.VMEM((ndev, 1, 128), jnp.float32),
            pltpu.VMEM((NOWN * 16, ndev * 32), bf16),
            pltpu.VMEM((CHUNKS, NEXT, TOK, C), bf16),
            pltpu.VMEM((8, NOWN, TILE, 128), bf16),
            pltpu.VMEM((8, NEXT, TILE, 128), bf16),
            pltpu.VMEM((8, NEXT, TILE, 128), bf16),
            pltpu.SemaphoreType.DMA((6,)),
            pltpu.SemaphoreType.DMA((CHUNKS, 4)),
            pltpu.SemaphoreType.DMA((CHUNKS,)),
            pltpu.SemaphoreType.DMA((CHUNKS,)),
            pltpu.SemaphoreType.DMA,
            pltpu.SemaphoreType.DMA,
            pltpu.SemaphoreType.DMA((CHUNKS,)),
            pltpu.SemaphoreType.DMA((CHUNKS,)),
        ],
        compiler_params=pltpu.CompilerParams(
            collective_id=0, has_side_effects=True, vmem_limit_bytes=63 << 20),
    )(item, valid, ids, gain, *tables, cells, weights, we, wq, wk, wv)


def attend_kernel(idx_ref, q_ref, k_ref, v_ref, rem_ref, we_ref, wo_ref, out_ref, att_scr, s_scr):
    pair = pl.program_id(0)
    first = lax.broadcasted_iota(jnp.int32, (1, 128), 1) < 64
    ones = jnp.ones((9 * TILE, 128), jnp.bfloat16)
    zero = jnp.zeros((TILE, 128), jnp.bfloat16)

    def scores(t, slot):
        q = q_ref[0, t]
        both = jnp.concatenate([jnp.where(first, q, zero), jnp.where(first, zero, q)], axis=0)
        for j in range(9):
            s_scr[slot, :, j * TILE:(j + 1) * TILE] = lax.dot_general(
                both, k_ref[0, idx_ref[t * 9 + j]], (((1,), (1,)), ((), ())),
                preferred_element_type=jnp.float32)

    def combine(t, slot):
        s = s_scr[slot]
        m = jnp.max(s, axis=-1, keepdims=True)
        w = jnp.exp(s - m).astype(jnp.bfloat16)
        near = jnp.concatenate([v_ref[0, idx_ref[t * 9 + j]] for j in range(9)], axis=0)
        o = jnp.dot(w, jnp.concatenate([near, ones], axis=1), preferred_element_type=jnp.float32)
        o = o[:, :128] / o[:, 128:]
        att_scr[pair, t] = jnp.where(first, o[:TILE], o[TILE:]).astype(jnp.bfloat16)

    scores(0, 0)

    def step(half, carry):
        t = half * 2
        scores(t + 1, 1)
        combine(t, 0)
        scores(jnp.minimum(t + 2, NOWN - 1), 0)
        combine(t + 1, 1)
        return carry

    lax.fori_loop(0, NOWN // 2, step, 0)

    @pl.when(pair == 7)
    def _():
        def finish(g, carry):
            base = g * 4
            rows = 4 * TILE
            att = jnp.concatenate(
                [att_scr[p, pl.ds(base, 4)].reshape(rows, 128) for p in range(8)]
                + [rem_ref[pl.ds(base, 4)].reshape(rows, 128)], axis=1)
            for n in range(4):
                cols = slice(n * 256, (n + 1) * 256)
                o = jnp.dot(att[:, :D], wo_ref[:, cols], preferred_element_type=jnp.float32)
                o = o + jnp.dot(att[:, D:], we_ref[:, cols], preferred_element_type=jnp.float32)
                out_ref[pl.ds(base, 4), :, cols] = o.astype(jnp.bfloat16).reshape(4, TILE, 256)
            return carry

        lax.fori_loop(0, NOWN // 4, finish, 0)


def attend(idx, q, k, v, rem, we, wo):
    whole = lambda shape: pl.BlockSpec(shape, lambda p: (0,) * len(shape), pipeline_mode=pl.Buffered(1))
    slab = lambda n: pl.BlockSpec((1, n, TILE, 128), lambda p: (p, 0, 0, 0))
    return pl.pallas_call(
        attend_kernel,
        grid=(8,),
        out_shape=jax.ShapeDtypeStruct((NOWN, TILE, D), jnp.bfloat16),
        in_specs=[
            pl.BlockSpec(memory_space=pltpu.SMEM), slab(NOWN), slab(NEXT), slab(NEXT),
            whole((NOWN, TILE, 128)), whole((128, D)), whole((D, D)),
        ],
        out_specs=whole((NOWN, TILE, D)),
        scratch_shapes=[
            pltpu.VMEM((8, NOWN, TILE, 128), jnp.bfloat16),
            pltpu.VMEM((2, 2 * TILE, 9 * TILE), jnp.float32),
        ],
        compiler_params=pltpu.CompilerParams(vmem_limit_bytes=60 << 20),
    )(idx, q, k, v, rem, we, wo)

def slots(remap_dest, remap_tile, me, ndev):
    dest = remap_dest.reshape(-1)
    named = remap_tile.reshape(-1) + 1
    count = dest.shape[0]
    order = jnp.arange(count)[None, :]
    same = dest[None, :] == jnp.arange(ndev)[:, None]
    first = jnp.min(jnp.where(same, order, count), axis=1)
    last = jnp.max(jnp.where(same, order, -1), axis=1)
    second = jnp.where(last > first, last, count)
    pick = jnp.stack([first, second], axis=1)
    valid = pick < count
    ids = jnp.sum(jnp.where(pick[:, :, None] == order[None], named[None, None, :], 0), axis=2)
    lane = jnp.arange(128)
    mine = (lane >> 5) == (me & 3)
    lanes = jnp.where((lane & 16) == 0, ids[:, :1], ids[:, 1:])
    lanes = jnp.where(mine, lanes, 0).astype(jnp.float32)
    item = jnp.where(valid, pick, 0).reshape(-1)
    return item, valid.astype(jnp.float32).reshape(-1), lanes.reshape(ndev, 1, 128)


def tile_slots(neighbours, band_at, sect_at, ncols):
    r = neighbours // ncols - band_at * 2 + 1
    c = jnp.mod(neighbours % ncols - sect_at * 6 + 1, ncols)
    slot = (r - 1) * 6 + c - 1
    slot = jnp.where(r == 0, 11 + c, slot)
    slot = jnp.where(r == 3, 17 + c, slot)
    slot = jnp.where(c == 0, 24 + r, slot)
    return jnp.where(c == 7, 28 + r, slot)


def trig_tables(band_at, sect_at, nrows, ncols):
    rows = (band_at * 2 - 1 + jnp.arange(4)).astype(jnp.float32)
    cols = jnp.mod(sect_at * 6 - 1 + jnp.arange(8), ncols).astype(jnp.float32)
    across = jnp.arange(8).astype(jnp.float32)
    along = jnp.arange(16).astype(jnp.float32)
    theta = math.pi * (rows[:, None] + (across + 0.5) * 16.0 / 128) / nrows
    phi = 2.0 * math.pi * (cols[:, None] + (along + 0.5) / 16.0) / ncols
    lane = np.arange(128)
    freq = jnp.asarray((lane % 16 + 1).astype(np.float32))
    theta = theta[..., None] * freq
    phi = phi[..., None] * freq
    sign = jnp.asarray(np.where(lane % 32 < 16, -1.0, 1.0).astype(np.float32))
    return jnp.cos(theta), jnp.cos(phi), jnp.sin(theta) * sign, jnp.sin(phi) * sign


def body(
    grid_cells,
    remap_weight,
    remap_dest,
    remap_tile,
    w_embed,
    norm_gain,
    w_query,
    w_key,
    w_value,
    w_out,
    neighbours,
):
    nband = lax.axis_size("band")
    nsect = lax.axis_size("sector")
    ndev = nband * nsect
    blocks, top, rowcells, tile = remap_weight.shape
    trows, tcols = (neighbours.shape[0], neighbours.shape[1])
    owned = trows * tcols
    band_at = lax.axis_index("band")
    sect_at = lax.axis_index("sector")
    item, valid, ids = slots(remap_dest, remap_tile, band_at * nsect + sect_at, ndev)
    tables = trig_tables(band_at, sect_at, trows * nband, tcols * nsect)
    index = tile_slots(neighbours.reshape(owned, 9), band_at, sect_at, tcols * nsect).reshape(-1)
    rem, q, k, v = front(
        nband, nsect, item, valid, ids, norm_gain.reshape(1, -1), tables,
        grid_cells, remap_weight.reshape(blocks * top, rowcells, tile), w_embed, w_query, w_key, w_value,
    )
    result = attend(index, q, k, v, rem, w_embed, w_out)
    return result.reshape(trows, tcols, tile, -1)


def solution(mesh):
    return jax.shard_map(
        body,
        mesh=mesh,
        in_specs=(
            P(("band", "sector"), None, None),
            P(("band", "sector"), None, None, None),
            P(("band", "sector"), None),
            P(("band", "sector"), None),
            P(),
            P(),
            P(),
            P(),
            P(),
            P(),
            P("band", "sector", None),
        ),
        out_specs=P("band", "sector", None, None),
        check_vma=False,
    )
```

```python
import functools
import math

import jax
import jax.numpy as jnp
import numpy as np
from jax import lax
from jax.experimental import pallas as pl
from jax.experimental.pallas import tpu as pltpu
from jax.sharding import PartitionSpec as P

NOWN, NEXT, TILE, D, C = 12, 32, 128, 1024, 128
CHUNKS = 4
TOK = TILE // CHUNKS
STRIDE = 37

PLACES = (
    [(r, c) for r in (1, 2) for c in range(1, 7)]
    + [(0, c) for c in range(1, 7)]
    + [(3, c) for c in range(1, 7)]
    + [(r, 0) for r in range(4)]
    + [(r, 7) for r in range(4)]
)


def front_kernel(nband, nsect, item_ref, ids_ref, gain_ref, cos_ref, sin_ref,
                 cells_hbm, weight_hbm, we_hbm, wq_hbm, wk_hbm, wv_hbm,
                 rem_out, q_out, k_out, v_out,
                 cells_ref, weight_ref, we_ref, wq_ref, wk_ref, wv_ref,
                 send_scr, recv_scr, gids_scr, lhs_scr, rem_scr, q_scr, k_scr, v_scr,
                 load_sem, out_sem, send_sem, recv_sem, isend_sem, irecv_sem, hsend_sem, hrecv_sem):
    ndev = nband * nsect
    items = weight_hbm.shape[0]
    band, sect = lax.axis_index("band"), lax.axis_index("sector")
    me = band * nsect + sect
    mesh_id = pl.DeviceIdType.MESH
    loads = [
        pltpu.make_async_copy(src, dst, load_sem.at[i])
        for i, (src, dst) in enumerate((
            (cells_hbm, cells_ref), (weight_hbm, weight_ref), (we_hbm, we_ref),
            (wk_hbm, wk_ref), (wv_hbm, wv_ref), (wq_hbm, wq_ref)))
    ]
    loads[0].start()
    loads[1].start()
    barrier = pltpu.get_barrier_semaphore()

    def where_is(i):
        d = lax.rem(me + i * STRIDE, ndev)
        return d, (lax.div(d, nsect), lax.rem(d, nsect))

    def greet(i, carry):
        _, place = where_is(i)
        pl.semaphore_signal(barrier, inc=1, device_id=place, device_id_type=mesh_id)
        return carry

    lax.fori_loop(1, ndev, greet, 0)
    rem_scr[:, NOWN:] = jnp.zeros((CHUNKS, NEXT - NOWN, TOK, C), jnp.bfloat16)
    loads[0].wait()
    loads[1].wait()
    for load in loads[2:]:
        load.start()

    def fill(dst, slot, d):
        for k in range(2):
            slot_item = item_ref[2 * d + k]
            used = jnp.where(slot_item < items, 1.0, 0.0)
            item = jnp.minimum(slot_item, items - 1)
            value = lax.dot_general(weight_ref[item], cells_ref[item >> 1], (((0,), (0,)), ((), ())),
                                    preferred_element_type=jnp.float32)
            value = (value * used).astype(jnp.bfloat16)
            for h in range(CHUNKS):
                dst[h, slot, k] = value[h * TOK:(h + 1) * TOK]

    fill(recv_scr, me, me)
    gids_scr[me] = ids_ref[me]

    def make(i):
        d, _ = where_is(i)
        fill(send_scr, d, d)

    def ship(h, i):
        d, place = where_is(i)
        pltpu.make_async_remote_copy(
            src_ref=send_scr.at[h, d], dst_ref=recv_scr.at[h, me],
            send_sem=send_sem.at[h], recv_sem=recv_sem.at[h],
            device_id=place, device_id_type=mesh_id).start()

    def ship_first(i):
        d, place = where_is(i)
        pltpu.make_async_remote_copy(
            src_ref=ids_ref.at[d], dst_ref=gids_scr.at[me], send_sem=isend_sem, recv_sem=irecv_sem,
            device_id=place, device_id_type=mesh_id).start()
        ship(0, i)
        ship(1, i)

    def ship_all(h):
        lax.fori_loop(1, ndev, lambda i, c: (ship(h, i), c)[1], 0)

    make(1)
    make(2)
    pl.semaphore_wait(barrier, ndev - 1)

    def step(i, carry):
        make(i + 2)
        ship_first(i)
        return carry

    lax.fori_loop(1, ndev - 2, step, 0)
    ship_first(ndev - 2)
    ship_first(ndev - 1)
    ship_all(2)

    others = pl.ds(0, ndev - 1)
    pltpu.make_async_copy(gids_scr.at[others], gids_scr.at[others], irecv_sem).wait()
    lane = lax.broadcasted_iota(jnp.int32, (NOWN * 16, 128), 1)
    row = lax.broadcasted_iota(jnp.int32, (NOWN * 16, 128), 0)
    diag = (lane & 15) == (row & 15)
    want = ((row >> 4) + 1).astype(jnp.float32)
    for b in range(ndev // 4):
        named = gids_scr[4 * b] + gids_scr[4 * b + 1] + gids_scr[4 * b + 2] + gids_scr[4 * b + 3]
        hit = jnp.where(diag & (named == want), 1.0, 0.0)
        lhs_scr[:, b * 128:(b + 1) * 128] = hit.astype(jnp.bfloat16)
    for load in loads[2:]:
        load.wait()

    lane = lax.broadcasted_iota(jnp.int32, (1, 128), 1)
    is_row = (lane & 63) < 32
    is_low = (lane & 31) < 16

    north = jnp.maximum(band - 1, 0)
    south = jnp.minimum(band + 1, nband - 1)
    west = lax.rem(sect + nsect - 1, nsect)
    east = lax.rem(sect + 1, nsect)

    def halo(h):
        def send(src, dst, count, place):
            pltpu.make_async_remote_copy(
                src_ref=rem_scr.at[h, pl.ds(src, count)], dst_ref=rem_scr.at[h, pl.ds(dst, count)],
                send_sem=hsend_sem.at[h], recv_sem=hrecv_sem.at[h],
                device_id=place, device_id_type=mesh_id).start()

        send(0, 29, 1, (band, west))
        send(6, 30, 1, (band, west))
        send(5, 25, 1, (band, east))
        send(11, 26, 1, (band, east))

        @pl.when(band > 0)
        def _():
            send(0, 18, 6, (north, sect))
            send(0, 31, 1, (north, west))
            send(5, 27, 1, (north, east))

        @pl.when(band < nband - 1)
        def _():
            send(6, 12, 6, (south, sect))
            send(6, 28, 1, (south, west))
            send(11, 24, 1, (south, east))

    def halo_wait(h, sem):
        def wait(count):
            ref = rem_scr.at[h, pl.ds(0, count)]
            pltpu.make_async_copy(ref, ref, sem).wait()

        inner = (band > 0) & (band < nband - 1)

        @pl.when(inner)
        def _():
            wait(20)

        @pl.when(jnp.logical_not(inner))
        def _():
            wait(12)

    def project(h, base, count):
        rows = count * TOK
        toks = pl.ds(h * TOK, TOK)
        tiles = slice(base, base + count)
        places = PLACES[base:base + count]
        def spread(table):
            blocks = []
            for r, c in places:
                for g in range(TOK // 16):
                    line = table[pl.ds(r * 8 + h * (TOK // 16) + g, 1), :]
                    blocks.append(jnp.where(is_row, line, table[32 + c * 16:48 + c * 16, :]))
            return jnp.concatenate(blocks, axis=0)

        cos, sin = spread(cos_ref), spread(sin_ref)

        def rotary(u):
            partner = jnp.where(is_low, pltpu.roll(u, 112, 1), pltpu.roll(u, 16, 1))
            return u * cos + partner * sin

        rem = rem_scr[h, tiles].reshape(rows, C)
        emb = jnp.dot(rem, we_ref[...], preferred_element_type=jnp.float32)
        ms = jnp.mean(emb * emb, axis=-1, keepdims=True)
        normed = (emb * lax.rsqrt(ms + 1e-05) * gain_ref[...]).astype(jnp.bfloat16)

        def put(dst, pair, value):
            dst[pair, tiles, toks, :] = value.reshape(count, TOK, 128)

        for n in range(4):
            cols = slice(n * 256, (n + 1) * 256)
            k = jnp.dot(normed, wk_ref[:, cols], preferred_element_type=jnp.float32)
            v = jnp.dot(normed, wv_ref[:, cols], preferred_element_type=jnp.float32)
            for p in range(2):
                half = slice(p * 128, (p + 1) * 128)
                put(k_scr, 2 * n + p, rotary(k[:, half]).astype(jnp.bfloat16))
                put(v_scr, 2 * n + p, v[:, half].astype(jnp.bfloat16))
            if base < NOWN:
                q = jnp.dot(normed, wq_ref[:, cols], preferred_element_type=jnp.float32)
                for p in range(2):
                    half = slice(p * 128, (p + 1) * 128)
                    turned = rotary(q[:, half]).astype(jnp.bfloat16)
                    put(q_scr, 2 * n + p, turned * jnp.asarray(0.125, jnp.bfloat16))

    def outs(h, own):
        toks = pl.ds(h * TOK, TOK)
        tiles = pl.ds(0, NOWN) if own else pl.ds(NOWN, NEXT - NOWN)
        pairs = [(s.at[:, tiles, toks, :], o.at[:, tiles, toks, :]) for s, o in ((k_scr, k_out), (v_scr, v_out))]
        if own:
            pairs.append((q_scr.at[:, :, toks, :], q_out.at[:, :, toks, :]))
            pairs.append((rem_scr.at[h, tiles], rem_out.at[:, toks, :]))
        first = 0 if own else 4
        return [pltpu.make_async_copy(s, o, out_sem.at[h, first + i]) for i, (s, o) in enumerate(pairs)]

    pending = []

    def flush():
        for copies in pending:
            for copy in copies:
                copy.start()
        pending.clear()

    def own_part(h):
        pltpu.make_async_copy(recv_scr.at[h, others], recv_scr.at[h, others], recv_sem.at[h]).wait()
        for b in range(TOK // 32):
            low = recv_scr[h, :, :, b * 32:b * 32 + 16, :].reshape(ndev * 32, 128)
            high = recv_scr[h, :, :, b * 32 + 16:b * 32 + 32, :].reshape(ndev * 32, 128)
            total = jnp.dot(lhs_scr[...], jnp.concatenate([low, high], axis=1),
                            preferred_element_type=jnp.float32).astype(jnp.bfloat16)
            for l in range(NOWN):
                rem_scr[h, l, b * 32:b * 32 + 16, :] = total[l * 16:(l + 1) * 16, :128]
                rem_scr[h, l, b * 32 + 16:b * 32 + 32, :] = total[l * 16:(l + 1) * 16, 128:]
        flush()
        halo(h)
        if h == 0:
            ship_all(3)
        project(h, 0, NOWN)
        pending.append(outs(h, True))

    def halo_part(h):
        halo_wait(h, hrecv_sem.at[h])
        project(h, NOWN, NEXT - NOWN)
        flush()
        pending.append(outs(h, False))

    own_part(0)
    own_part(1)
    own_part(2)
    halo_part(0)
    own_part(3)
    halo_part(1)
    halo_part(2)
    halo_part(3)
    flush()
    pltpu.make_async_copy(ids_ref.at[others], ids_ref.at[others], isend_sem).wait()
    for h in range(CHUNKS):
        pltpu.make_async_copy(send_scr.at[h, others], send_scr.at[h, others], send_sem.at[h]).wait()
        halo_wait(h, hsend_sem.at[h])
        for copy in outs(h, True) + outs(h, False):
            copy.wait()


def front(nband, nsect, item, ids, gain, tables, cells, weights, we, wq, wk, wv):
    ndev = nband * nsect
    smem = pl.BlockSpec(memory_space=pltpu.SMEM)
    vmem = pl.BlockSpec(memory_space=pltpu.VMEM)
    hbm = pl.BlockSpec(memory_space=pltpu.HBM)
    bf16 = jnp.bfloat16
    items, blocks = weights.shape[0], cells.shape[0]
    return pl.pallas_call(
        functools.partial(front_kernel, nband, nsect),
        out_shape=[
            jax.ShapeDtypeStruct((NOWN, TILE, C), bf16),
            jax.ShapeDtypeStruct((8, NOWN, TILE, 128), bf16),
            jax.ShapeDtypeStruct((8, NEXT, TILE, 128), bf16),
            jax.ShapeDtypeStruct((8, NEXT, TILE, 128), bf16),
        ],
        in_specs=[smem] + [vmem] * 4 + [hbm] * 6,
        out_specs=[hbm] * 4,
        scratch_shapes=[
            pltpu.VMEM((blocks, 128, C), bf16),
            pltpu.VMEM((items, 128, TILE), bf16),
            pltpu.VMEM((C, D), bf16),
            pltpu.VMEM((D, D), bf16),
            pltpu.VMEM((D, D), bf16),
            pltpu.VMEM((D, D), bf16),
            pltpu.VMEM((CHUNKS, ndev, 2, TOK, C), bf16),
            pltpu.VMEM((CHUNKS, ndev, 2, TOK, C), bf16),
            pltpu.VMEM((ndev, 1, 128), jnp.float32),
            pltpu.VMEM((NOWN * 16, ndev * 32), bf16),
            pltpu.VMEM((CHUNKS, NEXT, TOK, C), bf16),
            pltpu.VMEM((8, NOWN, TILE, 128), bf16),
            pltpu.VMEM((8, NEXT, TILE, 128), bf16),
            pltpu.VMEM((8, NEXT, TILE, 128), bf16),
            pltpu.SemaphoreType.DMA((6,)),
            pltpu.SemaphoreType.DMA((CHUNKS, 6)),
            pltpu.SemaphoreType.DMA((CHUNKS,)),
            pltpu.SemaphoreType.DMA((CHUNKS,)),
            pltpu.SemaphoreType.DMA,
            pltpu.SemaphoreType.DMA,
            pltpu.SemaphoreType.DMA((CHUNKS,)),
            pltpu.SemaphoreType.DMA((CHUNKS,)),
        ],
        compiler_params=pltpu.CompilerParams(
            collective_id=0, has_side_effects=True, vmem_limit_bytes=63 << 20),
    )(item, ids, gain, *tables, cells, weights, we, wq, wk, wv)


def attend_kernel(idx_ref, q_ref, k_ref, v_ref, rem_ref, we_ref, wo_ref, out_ref, att_scr, s_scr):
    pair = pl.program_id(0)
    first = lax.broadcasted_iota(jnp.int32, (1, 128), 1) < 64
    ones = jnp.ones((9 * TILE, 128), jnp.bfloat16)
    zero = jnp.zeros((TILE, 128), jnp.bfloat16)

    def scores(t, slot):
        q = q_ref[0, t]
        both = jnp.concatenate([jnp.where(first, q, zero), jnp.where(first, zero, q)], axis=0)
        for j in range(9):
            s_scr[slot, :, j * TILE:(j + 1) * TILE] = lax.dot_general(
                both, k_ref[0, idx_ref[t * 9 + j]], (((1,), (1,)), ((), ())),
                preferred_element_type=jnp.float32)

    def combine(t, slot):
        s = s_scr[slot]
        m = jnp.max(s, axis=-1, keepdims=True)
        w = jnp.exp(s - m).astype(jnp.bfloat16)
        near = jnp.concatenate([v_ref[0, idx_ref[t * 9 + j]] for j in range(9)], axis=0)
        o = jnp.dot(w, jnp.concatenate([near, ones], axis=1), preferred_element_type=jnp.float32)
        o = o[:, :128] / o[:, 128:]
        att_scr[pair, t] = jnp.where(first, o[:TILE], o[TILE:]).astype(jnp.bfloat16)

    scores(0, 0)

    def step(half, carry):
        t = half * 2
        scores(t + 1, 1)
        combine(t, 0)
        scores(jnp.minimum(t + 2, NOWN - 1), 0)
        combine(t + 1, 1)
        return carry

    lax.fori_loop(0, NOWN // 2, step, 0)

    @pl.when(pair == 7)
    def _():
        def finish(g, carry):
            base = g * 4
            rows = 4 * TILE
            att = jnp.concatenate(
                [att_scr[p, pl.ds(base, 4)].reshape(rows, 128) for p in range(8)]
                + [rem_ref[pl.ds(base, 4)].reshape(rows, 128)], axis=1)
            for n in range(4):
                cols = slice(n * 256, (n + 1) * 256)
                o = jnp.dot(att[:, :D], wo_ref[:, cols], preferred_element_type=jnp.float32)
                o = o + jnp.dot(att[:, D:], we_ref[:, cols], preferred_element_type=jnp.float32)
                out_ref[pl.ds(base, 4), :, cols] = o.astype(jnp.bfloat16).reshape(4, TILE, 256)
            return carry

        lax.fori_loop(0, NOWN // 4, finish, 0)


def attend(idx, q, k, v, rem, we, wo):
    whole = lambda shape: pl.BlockSpec(shape, lambda p: (0,) * len(shape), pipeline_mode=pl.Buffered(1))
    slab = lambda n: pl.BlockSpec((1, n, TILE, 128), lambda p: (p, 0, 0, 0))
    return pl.pallas_call(
        attend_kernel,
        grid=(8,),
        out_shape=jax.ShapeDtypeStruct((NOWN, TILE, D), jnp.bfloat16),
        in_specs=[
            pl.BlockSpec(memory_space=pltpu.SMEM), slab(NOWN), slab(NEXT), slab(NEXT),
            whole((NOWN, TILE, 128)), whole((128, D)), whole((D, D)),
        ],
        out_specs=whole((NOWN, TILE, D)),
        scratch_shapes=[
            pltpu.VMEM((8, NOWN, TILE, 128), jnp.bfloat16),
            pltpu.VMEM((2, 2 * TILE, 9 * TILE), jnp.float32),
        ],
        compiler_params=pltpu.CompilerParams(vmem_limit_bytes=60 << 20),
    )(idx, q, k, v, rem, we, wo)

def slots(remap_dest, remap_tile, me, ndev):
    dest = remap_dest.reshape(-1)
    named = remap_tile.reshape(-1) + 1
    count = dest.shape[0]
    order = jnp.arange(count)[None, :]
    same = dest[None, :] == jnp.arange(ndev)[:, None]
    first = jnp.min(jnp.where(same, order, count), axis=1)
    last = jnp.max(jnp.where(same, order, -1), axis=1)
    second = jnp.where(last > first, last, count)
    pick = jnp.stack([first, second], axis=1)
    ids = jnp.sum(jnp.where(pick[:, :, None] == order[None], named[None, None, :], 0), axis=2)
    lane = jnp.arange(128)
    mine = (lane >> 5) == (me & 3)
    lanes = jnp.where((lane & 16) == 0, ids[:, :1], ids[:, 1:])
    lanes = jnp.where(mine, lanes, 0).astype(jnp.float32)
    return pick.reshape(-1), lanes.reshape(ndev, 1, 128)


def tile_slots(neighbours, band_at, sect_at, ncols):
    past = neighbours - (band_at * 2 - 1) * ncols
    r = jnp.zeros_like(past)
    for edge in range(1, 4):
        r = r + (past >= edge * ncols).astype(jnp.int32)
    c = past - r * ncols - (sect_at * 6 - 1)
    c = jnp.where(c < 0, c + ncols, jnp.where(c >= ncols, c - ncols, c))
    slot = (r - 1) * 6 + c - 1
    slot = jnp.where(r == 0, 11 + c, slot)
    slot = jnp.where(r == 3, 17 + c, slot)
    slot = jnp.where(c == 0, 24 + r, slot)
    return jnp.where(c == 7, 28 + r, slot)


def trig_tables(band_at, sect_at, nrows, ncols):
    line = jnp.arange(160)[:, None]
    lane = jnp.arange(128)[None, :]
    freq = ((lane & 15) + 1).astype(jnp.float32)
    row = (band_at * 2 - 1 + (line >> 3)).astype(jnp.float32)
    across = (line & 7).astype(jnp.float32)
    theta = math.pi * (row + (across + 0.5) * 16.0 / 128) / nrows
    col = sect_at * 6 - 1 + ((line - 32) >> 4)
    col = jnp.where(col < 0, col + ncols, jnp.where(col >= ncols, col - ncols, col)).astype(jnp.float32)
    along = (line & 15).astype(jnp.float32)
    phi = 2.0 * math.pi * (col + (along + 0.5) / 16.0) / ncols
    angle = jnp.where(line < 32, theta, phi) * freq
    sign = jnp.where((lane & 31) < 16, -1.0, 1.0)
    return jnp.cos(angle), jnp.sin(angle) * sign


def body(
    grid_cells,
    remap_weight,
    remap_dest,
    remap_tile,
    w_embed,
    norm_gain,
    w_query,
    w_key,
    w_value,
    w_out,
    neighbours,
):
    nband = lax.axis_size("band")
    nsect = lax.axis_size("sector")
    ndev = nband * nsect
    blocks, top, rowcells, tile = remap_weight.shape
    trows, tcols = (neighbours.shape[0], neighbours.shape[1])
    owned = trows * tcols
    band_at = lax.axis_index("band")
    sect_at = lax.axis_index("sector")
    item, ids = slots(remap_dest, remap_tile, band_at * nsect + sect_at, ndev)
    tables = trig_tables(band_at, sect_at, trows * nband, tcols * nsect)
    index = tile_slots(neighbours.reshape(owned, 9), band_at, sect_at, tcols * nsect).reshape(-1)
    rem, q, k, v = front(
        nband, nsect, item, ids, norm_gain.reshape(1, -1), tables,
        grid_cells, remap_weight.reshape(blocks * top, rowcells, tile), w_embed, w_query, w_key, w_value,
    )
    result = attend(index, q, k, v, rem, w_embed, w_out)
    return result.reshape(trows, tcols, tile, -1)


def solution(mesh):
    return jax.shard_map(
        body,
        mesh=mesh,
        in_specs=(
            P(("band", "sector"), None, None),
            P(("band", "sector"), None, None, None),
            P(("band", "sector"), None),
            P(("band", "sector"), None),
            P(),
            P(),
            P(),
            P(),
            P(),
            P(),
            P("band", "sector", None),
        ),
        out_specs=P("band", "sector", None, None),
        check_vma=False,
    )
```
